32 devices in a mesh: dp: 4 (over y, x), seq: 2 (over core), head: 4 (over z).
Axes of the slice: x: 2, y: 2, z: 4, core: 2. Of those that a mesh axis runs over, the one named last changes fastest.
Arguments:
- tokens: bfloat16 [4, 1024, 2048], P('dp', 'seq'), may hold values from -6 to 6
- attn_gain: float32 [2048], replicated, may hold values from 0.1 to 1.9
- w_qkvg: bfloat16 [4, 2048, 2048], P(None, None, 'head'), may hold values from -0.125 to 0.125
- w_beta: bfloat16 [2048, 16], P(None, 'head'), may hold values from -0.25 to 0.25
- conv_w: float32 [3, 4, 2048], P(None, None, 'head'), may hold values from -3 to 3
- out_gain: float32 [128], replicated, may hold values from 0.1 to 1.9
- w_o: bfloat16 [2048, 2048], P('head'), may hold values from -0.125 to 0.125
- mlp_gain: float32 [2048], replicated, may hold values from 0.1 to 1.9
- w_gateup: bfloat16 [2, 2048, 5632], P(None, None, 'head'), may hold values from -0.125 to 0.125
- w_down: bfloat16 [5632, 2048], P('head'), may hold values from -0.078125 to 0.078125
- cotangent: bfloat16 [4, 1024, 2048], P('dp', 'seq'), may hold values from -6 to 6
Outputs:
- out: bfloat16 [4, 1024, 2048], P('dp', 'seq')
- grad_tokens: bfloat16 [4, 1024, 2048], P('dp', 'seq')
- grad_attn_gain: float32 [2048], replicated
- grad_w_qkvg: float32 [4, 2048, 2048], P(None, ('dp', 'seq'), 'head')
- grad_w_beta: float32 [2048, 16], P(None, 'head')
- grad_conv_w: float32 [3, 4, 2048], P(None, None, 'head')
- grad_out_gain: float32 [128], replicated
- grad_w_o: float32 [2048, 2048], P('head', ('dp', 'seq'))
- grad_mlp_gain: float32 [2048], replicated
- grad_w_gateup: float32 [2, 2048, 5632], P(None, ('dp', 'seq'), 'head')
- grad_w_down: float32 [5632, 2048], P('head', ('dp', 'seq'))
- state_mean: float32 [], replicated
The draws below stay inside these ranges and needn't reach their ends.
All inputs are finite; a program needn't handle non-finite values.
Results may differ from the reference program's by a relative error of at most 0.012.
The reference program's roundings to bfloat16 on the way count: a program that leaves them out, or rounds other values in their place, can miss the bound.
Values may be sent and summed in bfloat16 or wider, within the bound.
A program may use at most 320 MiB of HBM per device.

```python
import jax
import jax.numpy as jnp
from jax import lax

D = 2048
H = 16
HD = 128
FF = 5632
KCONV = 4
SPAN = 64
TOK_DEV = 512
LEN = 1024
SEQS = 4


def spiked(values, rng, source, target, shards_of, factor):
    owner, partner = [(jnp.arange(values.shape[dim]) // (values.shape[dim] // shards_of)).reshape([-1 if axis == dim else 1 for axis in range(values.ndim)]) for dim in (source, target)]
    chosen = jax.random.permutation(rng, shards_of)[partner]
    strong = (owner == chosen) | (owner == (partner + shards_of // 2) % shards_of)
    return jnp.where(strong, factor * values, values)


def block_scale(stream_key, shape, shards, low, largest):
    def one(dim, blocks):
        draws = jax.random.uniform(jax.random.fold_in(jax.random.fold_in(stream_key, 6), dim), (blocks,), jnp.float32, low / len(shards), largest / len(shards))
        return jnp.repeat(jnp.exp(draws), shape[dim] // blocks).reshape((-1,) + (1,) * (len(shape) - dim - 1))

    factor_of = one(*shards[0])
    for cut in shards[1:]:
        factor_of = factor_of * one(*cut)
    return factor_of


def normal_values(own_key, dims, scale, most, cuts=(), held_as=jnp.bfloat16):
    values = jax.random.normal(own_key, dims, jnp.float32) * scale
    if len(cuts) > 0:
        values = block_scale(own_key, dims, cuts, -0.22, 0.18) * values
    return jnp.clip(values, min=-most, max=most).astype(held_as)


def gaussian_with(key, extent, scale, reach, cuts, heavy, kind=jnp.bfloat16):
    entries = scale * jax.random.normal(key, extent, jnp.float32)
    if cuts:
        entries = entries * block_scale(key, extent, cuts, -0.22, 0.18)
    return jnp.clip(spiked(entries, jax.random.fold_in(key, 3), *heavy), -reach, reach).astype(kind)


def setup_inputs(seed: int = 0) -> dict:
    key_of = jax.random.split(jax.random.key(seed), 12)
    return {
        "tokens": gaussian_with(key_of[0], (SEQS, LEN, D), 1.0, 6.0, ((0, 4), (1, 2)), (1, 2, 2, 2.0)),
        "attn_gain": jnp.clip(1.0 + 0.18 * jax.random.normal(key_of[1], (D,), jnp.float32), 0.1, 1.9),
        "w_qkvg": normal_values(key_of[2], (4, D, D), D ** -0.5, 0.125, ((2, 4),)),
        "w_beta": normal_values(key_of[3], (D, H), (D // 4) ** -0.5, 0.25, ((1, 4),)),
        "conv_w": normal_values(key_of[4], (3, KCONV, D), KCONV ** -0.5, 3.0, ((2, 4),), jnp.float32),
        "out_gain": jnp.clip(1.0 + 0.18 * jax.random.normal(key_of[5], (HD,), jnp.float32), 0.1, 1.9),
        "w_o": normal_values(key_of[6], (D, D), D ** -0.5, 0.125, ((0, 4),)),
        "mlp_gain": jnp.clip(1.0 + 0.18 * jax.random.normal(key_of[7], (D,), jnp.float32), 0.1, 1.9),
        "w_gateup": normal_values(key_of[8], (2, D, FF), D ** -0.5, 0.125, ((2, 4),)),
        "w_down": normal_values(key_of[9], (FF, D), FF ** -0.5, 0.078125, ((0, 4),)),
        "cotangent": gaussian_with(key_of[10], (SEQS, LEN, D), 1.0, 6.0, ((0, 4), (1, 2)), (1, 2, 2, 2.0)),
    }


@jax.custom_vjp
def low(v):
    return lax.optimization_barrier(v.astype(jnp.bfloat16)).astype(jnp.float32)

@jax.custom_vjp
def low_back(v):
    return v

def low_keep(v):
    return (low(v), None)

def low_pass(kept, grad):
    return (grad,)

def back_keep(v):
    return (v, None)

def back_low(kept, grad):
    return (low(grad),)
low.defvjp(low_keep, low_pass)
low_back.defvjp(back_keep, back_low)
FULL_PRECISION = lax.Precision.HIGHEST

def rms_scale(values, gain_vec):
    return values * lax.rsqrt(lax.optimization_barrier(jnp.mean(values * values, axis=-1, keepdims=True)) + 1e-06) * gain_vec

def unit_rows(values):
    return values * lax.rsqrt(lax.optimization_barrier(jnp.sum(values * values, axis=-1, keepdims=True)) + 1e-06)

def span_step(running_state, pieces):
    query_vectors, key_vectors, value_rows, beta_rows = pieces
    span_len = query_vectors.shape[1]
    scaled = key_vectors * beta_rows[..., None]
    gram_block = jnp.einsum('hik,hjk->hij', scaled, key_vectors, precision=FULL_PRECISION)
    system = jnp.eye(span_len, dtype=jnp.float32) + jnp.tril(gram_block, -1)
    householder_keys = jax.scipy.linalg.solve_triangular(system, scaled, lower=True, unit_diagonal=True)
    householder_values = jax.scipy.linalg.solve_triangular(system, value_rows * beta_rows[..., None], lower=True, unit_diagonal=True)
    update_rows = householder_values - jnp.einsum('nij,njq->niq', householder_keys, running_state, precision=FULL_PRECISION)
    causal = jnp.tril(jnp.ones((span_len, span_len), jnp.float32))
    attention_logits = jnp.einsum('hik,hjk->hij', query_vectors, key_vectors, precision=FULL_PRECISION) * causal
    block_results = jnp.einsum('nij,njq->niq', query_vectors, running_state, precision=FULL_PRECISION) + jnp.einsum('qkw,qwu->qku', attention_logits, update_rows, precision=FULL_PRECISION)
    next_segment = running_state + jnp.einsum('xea,xef->xaf', key_vectors, update_rows, precision=FULL_PRECISION)
    return (next_segment, (block_results, jnp.sqrt(lax.optimization_barrier(jnp.sum(next_segment * next_segment, axis=(1, 2))))))

def forward(tok_rows, attn_gain, w_qkvg, w_beta, conv_w, out_gain, w_o, mlp_gain, w_gateup, w_down):
    length = tok_rows.shape[0]
    normed = low(rms_scale(tok_rows, attn_gain))
    projected = jnp.einsum('td,cde->tce', normed, w_qkvg, precision=FULL_PRECISION)
    raw_proj = low_back(low(projected[:, :3]))
    gate_pre = low_back(projected[:, 3])
    beta_all = jax.nn.sigmoid(low_back(jnp.dot(normed, w_beta, precision=FULL_PRECISION)))
    padded = jnp.concatenate([jnp.zeros((KCONV - 1, 3, D), jnp.float32), raw_proj], axis=0)
    conv_sum = conv_w[:, 0] * padded[0:length]
    for tap_index in range(1, KCONV):
        conv_sum = conv_sum + conv_w[:, tap_index] * padded[tap_index:tap_index + length]
    active = jax.nn.silu(conv_sum)
    queries = unit_rows(active[:, 0].reshape(length, H, HD)) * HD ** (-0.5)
    key_vectors = unit_rows(active[:, 1].reshape(length, H, HD))
    value_rows = active[:, 2].reshape(length, H, HD)
    blocks = length // SPAN

    def to_blocks(values):
        return values.reshape(blocks, SPAN, H, HD).transpose(0, 2, 1, 3)
    beta_blocks = beta_all.reshape(blocks, SPAN, H).transpose(0, 2, 1)
    zero_state = jnp.zeros((H, HD, HD), jnp.float32)
    _, (outputs, state_norms) = lax.scan(jax.checkpoint(span_step), zero_state, (to_blocks(queries), to_blocks(key_vectors), to_blocks(value_rows), beta_blocks))
    outputs = outputs.transpose(0, 2, 1, 3).reshape(length, H, HD)
    gate_heads = gate_pre.reshape(length, H, HD)
    gated_rows = outputs * lax.rsqrt(lax.optimization_barrier(jnp.mean(outputs * outputs, axis=-1, keepdims=True)) + 1e-05) * out_gain * jax.nn.silu(gate_heads)
    gated_rows = low(gated_rows.reshape(length, D))
    hidden_state = tok_rows + low_back(jnp.dot(gated_rows, w_o, precision=FULL_PRECISION))
    normed_mlp = low(rms_scale(hidden_state, mlp_gain))
    gate_up = jnp.einsum('td,cdf->tcf', normed_mlp, w_gateup, precision=FULL_PRECISION)
    gate_act = low_back(gate_up[:, 0])
    up_act = low_back(gate_up[:, 1])
    hidden_units = low(jax.nn.silu(gate_act) * up_act)
    result = hidden_state + low_back(jnp.dot(hidden_units, w_down, precision=FULL_PRECISION))
    per_run = TOK_DEV // SPAN
    return (result, jnp.sum(state_norms[per_run - 1::per_run]))

def reference(tokens, attn_gain, w_qkvg, w_beta, conv_w, out_gain, w_o, mlp_gain, w_gateup, w_down, cotangent):
    params = (attn_gain, w_qkvg.astype(jnp.float32), w_beta.astype(jnp.float32), conv_w, out_gain, w_o.astype(jnp.float32), mlp_gain, w_gateup.astype(jnp.float32), w_down.astype(jnp.float32))

    def one_sequence(totals, pieces):
        seq_rows, seq_grad = pieces
        result, pullback, norm_sum = jax.vjp(forward, seq_rows.astype(jnp.float32), *params, has_aux=True)
        grad_list = pullback(seq_grad.astype(jnp.float32))
        totals = tuple((acc_total + grad_term for acc_total, grad_term in zip(totals, grad_list[1:])))
        return (totals, (result.astype(jnp.bfloat16), grad_list[0].astype(jnp.bfloat16), norm_sum))
    zero_totals = tuple((jnp.zeros_like(param_item) for param_item in params))
    totals, (outs_all, grad_all, norm_sums) = lax.scan(one_sequence, zero_totals, (tokens, cotangent))
    state_mean = jnp.sum(norm_sums) / (SEQS * (LEN // TOK_DEV) * H)
    return (outs_all, grad_all, totals[0], totals[1], totals[2], totals[3], totals[4], totals[5], totals[6], totals[7], totals[8], state_mean)
```

```python
import functools

import jax
import jax.numpy as jnp
from jax import lax
from jax.experimental import pallas as pl
from jax.experimental.pallas import tpu as pltpu
from jax.sharding import PartitionSpec as P

HD = 128
SPAN = 64
RIM = 16


MESH_ID = pl.DeviceIdType.MESH
F32 = jnp.float32
BF = jnp.bfloat16


def dot_nn(a, b):
    return lax.dot_general(a, b, (((1,), (0,)), ((), ())), preferred_element_type=F32)


def dot_nt(a, b):
    return lax.dot_general(a, b, (((1,), (1,)), ((), ())), preferred_element_type=F32)


def dot_tn(a, b):
    return lax.dot_general(a, b, (((0,), (0,)), ((), ())), preferred_element_type=F32)


def halves(a):
    high = a.astype(BF)
    return high, (a - high.astype(F32)).astype(BF)


def dot_fine(a, b, dot=dot_nn):
    a_high, a_rest = halves(a)
    b_high, b_rest = halves(b)
    return dot(a_high, b_high) + (dot(a_high, b_rest) + dot(a_rest, b_high))


def stack_heads(x, heads):
    return jnp.concatenate([x[:, h * HD : (h + 1) * HD] for h in range(heads)], axis=0)


def spread_heads(x, heads):
    return jnp.concatenate([x[h * SPAN : (h + 1) * SPAN] for h in range(heads)], axis=1)


def stack_column(x, heads):
    return jnp.concatenate(
        [jnp.broadcast_to(x[:, h : h + 1], (SPAN, HD)) for h in range(heads)], axis=0
    )


def sigmoid(x):
    return 1.0 / (1.0 + jnp.exp(-x))


def rows_of(b, count=SPAN):
    return pl.ds(pl.multiple_of(b * SPAN, SPAN), count)


def raw_window(raw, rim, c, b):
    now = raw[c, rows_of(b), :].astype(F32)
    start = pl.multiple_of(jnp.maximum(b * SPAN - RIM, 0), RIM)
    before = jnp.where(b == 0, rim[c].astype(F32), raw[c, pl.ds(start, RIM), :].astype(F32))
    return jnp.concatenate([before[RIM - 8 :], now], axis=0)


def shifted(window, j, taps):
    start = 8 - (taps - 1) + j
    return window[start : start + SPAN]


def meet(idx, count, axis):
    barrier = pltpu.get_barrier_semaphore()

    @pl.when(idx > 0)
    def _():
        pl.semaphore_signal(barrier, inc=1, device_id={axis: idx - 1}, device_id_type=MESH_ID)

    @pl.when(idx < count - 1)
    def _():
        pl.semaphore_signal(barrier, inc=1, device_id={axis: idx + 1}, device_id_type=MESH_ID)

    @pl.when(idx > 0)
    def _():
        pl.semaphore_wait(barrier, 1)

    @pl.when(idx < count - 1)
    def _():
        pl.semaphore_wait(barrier, 1)


def send_to(src, dst, send_sem, recv_sem, axis, target):
    return pltpu.make_async_remote_copy(
        src_ref=src,
        dst_ref=dst,
        send_sem=send_sem,
        recv_sem=recv_sem,
        device_id={axis: target},
        device_id_type=MESH_ID,
    )


def block_masks(heads):
    side = heads * SPAN
    row = lax.broadcasted_iota(jnp.int32, (side, side), 0)
    col = lax.broadcasted_iota(jnp.int32, (side, side), 1)
    same = (row // SPAN) == (col // SPAN)
    return row, col, same & (row > col), same & (row >= col)


def unit_lower_inverse(lower, row, col):
    inverse = jnp.where(row == col, 1.0, 0.0) - jnp.where((row // 2) == (col // 2), lower, 0.0)
    m = 2
    while m < SPAN:
        off = jnp.where(((row // (2 * m)) == (col // (2 * m))) & ((row // m) != (col // m)), lower, 0.0)
        inverse = inverse - dot_fine(dot_fine(inverse, off), inverse)
        m *= 2
    return inverse


def delta_forward_kernel(
    heads, runs, raw, conv_w, beta, gate, gain,
    gated, q_s, k_s, w_s, u_s, t_s, p_s, f_s, s_s, o_s, rim, norm,
    u_full, state, state_in, rim_in, rim_sems, state_sems,
):
    idx = lax.axis_index("seq")
    count_rows = raw.shape[1]
    taps = conv_w.shape[1]
    blocks = count_rows // SPAN
    last = count_rows - RIM
    if runs > 1:
        meet(idx, runs, "seq")

        @pl.when(idx < runs - 1)
        def _():
            send_to(raw.at[:, pl.ds(last, RIM), :], rim_in, rim_sems.at[0], rim_sems.at[1], "seq", idx + 1).start()

    row, col, strict, causal = block_masks(heads)

    def prepare_group(g, group):
        @pl.when(g == 0)
        def _():
            @pl.when(idx == 0)
            def _():
                rim[...] = jnp.zeros_like(rim)

            if runs > 1:
                @pl.when(idx > 0)
                def _():
                    send_to(rim_in, rim_in, rim_sems.at[0], rim_sems.at[1], "seq", idx - 1).wait_recv()
                    rim[...] = rim_in[...]

        for part in range(group):
            b = g * group + part
            parts = []
            for c in range(3):
                window = raw_window(raw, rim, c, b)
                taps_c = conv_w[c]
                mixed = taps_c[0:1] * shifted(window, 0, taps)
                for j in range(1, taps):
                    mixed = mixed + taps_c[j : j + 1] * shifted(window, j, taps)
                parts.append(stack_heads(mixed * sigmoid(mixed), heads))
            q, k, v = parts
            q = q * (lax.rsqrt(jnp.sum(q * q, axis=1, keepdims=True) + 1e-06) * HD ** (-0.5))
            k = k * lax.rsqrt(jnp.sum(k * k, axis=1, keepdims=True) + 1e-06)
            beta_c = stack_column(beta[rows_of(b), :], heads)
            scaled = k * beta_c
            lower = jnp.where(strict, dot_fine(scaled, k, dot_nt), 0.0)
            inverse = unit_lower_inverse(lower, row, col).astype(BF)
            k_low = k.astype(BF)
            q_low = q.astype(BF)
            wu = dot_nn(inverse, jnp.concatenate([scaled, v * beta_c], axis=1).astype(BF))
            attention = jnp.where(causal, dot_nt(q_low, k_low), 0.0)
            q_s[b] = q_low
            k_s[b] = k_low
            t_s[b] = inverse
            p_s[b] = attention.astype(BF)
            w_s[b] = wu[:, :HD].astype(BF)
            u_full[b] = wu[:, HD:]
            u_s[b] = wu[:, HD:].astype(BF)

    group = 2
    groups = blocks // group

    def prepare_loop(i, carry):
        prepare_group(groups - 1 - i, group)
        return carry

    lax.fori_loop(0, groups, prepare_loop, 0)

    @pl.when(idx == 0)
    def _():
        state[...] = jnp.zeros_like(state)

    if runs > 1:
        @pl.when(idx > 0)
        def _():
            send_to(state_in, state_in, state_sems.at[0], state_sems.at[1], "seq", idx - 1).wait_recv()
            state[...] = state_in[...]

    gain_row = gain[...]

    def scan_block(b, carry):
        fresh, out_part = [], []
        before = [state[h] for h in range(heads)]
        for h in range(heads):
            mine = pl.ds(h * SPAN, SPAN)
            low = before[h].astype(BF)
            s_s[b, h] = low
            both = dot_nn(jnp.concatenate([w_s[b, mine, :], q_s[b, mine, :]], axis=0), low)
            fresh.append(u_full[b, mine, :] - both[:SPAN])
            out_part.append(both[SPAN:])
        for h in range(heads):
            mine = pl.ds(h * SPAN, SPAN)
            state[h] = before[h] + dot_tn(k_s[b, mine, :], fresh[h].astype(BF))
        fresh_low = jnp.concatenate(fresh, axis=0).astype(BF)
        f_s[b] = fresh_low
        out = jnp.concatenate(out_part, axis=0) + dot_nn(p_s[b], fresh_low)
        o_s[b] = out
        g = stack_heads(gate[rows_of(b), :], heads)
        scale = lax.rsqrt(jnp.mean(out * out, axis=1, keepdims=True) + 1e-05)
        gated[rows_of(b), :] = spread_heads(out * scale * gain_row * (g * sigmoid(g)), heads).astype(BF)
        return carry

    lax.fori_loop(0, blocks, scan_block, 0)
    if runs > 1:
        @pl.when(idx < runs - 1)
        def _():
            send_to(state, state_in, state_sems.at[0], state_sems.at[1], "seq", idx + 1).start()

    total = jnp.zeros((1, HD), F32)
    for h in range(heads):
        end = state[h]
        square = jnp.sum(jnp.sum(end * end, axis=0, keepdims=True), axis=1, keepdims=True)
        total = total + jnp.broadcast_to(jnp.sqrt(square), (1, HD))
    norm[...] = jnp.broadcast_to(total, norm.shape)
    if runs > 1:
        @pl.when(idx < runs - 1)
        def _():
            send_to(raw.at[:, pl.ds(last, RIM), :], rim_in, rim_sems.at[0], rim_sems.at[1], "seq", idx + 1).wait_send()
            send_to(state, state_in, state_sems.at[0], state_sems.at[1], "seq", idx + 1).wait_send()


def delta_forward(raw, conv_w, beta, gate, gain, runs):
    count_rows, heads = beta.shape
    blocks = count_rows // SPAN
    side = heads * SPAN
    width = heads * HD
    sd = jax.ShapeDtypeStruct
    outs = [
        sd((count_rows, width), BF),
        sd((blocks, side, HD), BF),
        sd((blocks, side, HD), BF),
        sd((blocks, side, HD), BF),
        sd((blocks, side, HD), BF),
        sd((blocks, side, side), BF),
        sd((blocks, side, side), BF),
        sd((blocks, side, HD), BF),
        sd((blocks, heads, HD, HD), BF),
        sd((blocks, side, HD), F32),
        sd((3, RIM, width), BF),
        sd((8, HD), F32),
    ]
    vmem = pl.BlockSpec(memory_space=pltpu.VMEM)
    return pl.pallas_call(
        functools.partial(delta_forward_kernel, heads, runs),
        out_shape=outs,
        in_specs=[vmem] * 5,
        out_specs=[vmem] * len(outs),
        scratch_shapes=[
            pltpu.VMEM((blocks, side, HD), F32),
            pltpu.VMEM((heads, HD, HD), F32),
            pltpu.VMEM((heads, HD, HD), F32),
            pltpu.VMEM((3, RIM, width), BF),
            pltpu.SemaphoreType.DMA((2,)),
            pltpu.SemaphoreType.DMA((2,)),
        ],
        compiler_params=pltpu.CompilerParams(
            collective_id=0 if runs > 1 else None, has_side_effects=True, vmem_limit_bytes=48 << 20
        ),
        name="delta_forward",
    )(raw, conv_w, beta, gate, gain.reshape(1, HD))


def delta_backward_kernel(
    heads, runs, raw, rim, conv_w, beta, gate, gain,
    q_s, k_s, w_s, u_s, t_s, p_s, f_s, s_s, o_s, d_gated,
    d_raw, d_gate, d_beta, g_conv, g_gain,
    d_mixed, d_out, d_fresh, d_fresh0, q_out, after_s, state, state_in, edge_in, conv_acc, gain_acc,
    state_sems, edge_sems,
):
    idx = lax.axis_index("seq")
    count_rows = raw.shape[1]
    taps = conv_w.shape[1]
    blocks = count_rows // SPAN
    if runs > 1:
        meet(idx, runs, "seq")
    gain_row = gain[...]
    gain_acc[...] = jnp.zeros_like(gain_acc)
    conv_acc[...] = jnp.zeros_like(conv_acc)

    def gate_block(b, carry):
        o = o_s[b]
        g = stack_heads(gate[rows_of(b), :], heads)
        dg = stack_heads(d_gated[rows_of(b), :].astype(F32), heads)
        scale = lax.rsqrt(jnp.mean(o * o, axis=1, keepdims=True) + 1e-05)
        y = o * scale
        sig = sigmoid(g)
        silu = g * sig
        dgy = dg * y
        gain_acc[...] += jnp.sum((dgy * silu).reshape(-1, 8, HD), axis=0)
        d_gate[rows_of(b), :] = spread_heads(dgy * gain_row * (sig + silu * (1.0 - sig)), heads).astype(BF)
        dy = dg * gain_row * silu
        do = (scale * (dy - y * jnp.mean(dy * y, axis=1, keepdims=True))).astype(BF)
        d_out[b] = do
        d_fresh0[b] = dot_tn(p_s[b], do)
        for h in range(heads):
            mine = slice(h * SPAN, (h + 1) * SPAN)
            q_out[b, h] = dot_tn(q_s[b, mine, :], do[mine])
        return carry

    lax.fori_loop(0, blocks, gate_block, 0)

    @pl.when(idx == runs - 1)
    def _():
        state[...] = jnp.zeros_like(state)

    if runs > 1:
        @pl.when(idx < runs - 1)
        def _():
            send_to(state_in, state_in, state_sems.at[0], state_sems.at[1], "seq", idx + 1).wait_recv()
            state[...] = state_in[...]

    def scan_block(i, carry):
        b = blocks - 1 - i
        for h in range(heads):
            mine = pl.ds(h * SPAN, SPAN)
            after = state[h]
            low = after.astype(BF)
            after_s[b, h] = low
            df = (d_fresh0[b, mine, :] + dot_nn(k_s[b, mine, :], low)).astype(BF)
            d_fresh[b, mine, :] = df
            state[h] = after + q_out[b, h] - dot_tn(w_s[b, mine, :], df)
        return carry

    lax.fori_loop(0, blocks, scan_block, 0)
    if runs > 1:
        @pl.when(idx > 0)
        def _():
            send_to(state, state_in, state_sems.at[0], state_sems.at[1], "seq", idx - 1).start()

    row, col, strict, causal = block_masks(heads)
    lane = lax.broadcasted_iota(jnp.int32, (SPAN, HD), 1)

    def grad_block(b, carry):
        df = d_fresh[b]
        do = d_out[b]
        k_low = k_s[b]
        dw, dq, dk = [], [], []
        for h in range(heads):
            mine = slice(h * SPAN, (h + 1) * SPAN)
            both = dot_nt(jnp.concatenate([df[mine], do[mine]], axis=0), s_s[b, h])
            dw.append(-both[:SPAN])
            dq.append(both[SPAN:])
            dk.append(dot_nt(f_s[b, mine, :], after_s[b, h]))
        dw = jnp.concatenate(dw, axis=0)
        dp = jnp.where(causal, dot_nt(do, f_s[b]), 0.0).astype(BF)
        dq = jnp.concatenate(dq, axis=0) + dot_nn(dp, k_low)
        dk = jnp.concatenate(dk, axis=0) + dot_tn(dp, q_s[b])
        dx = dot_tn(t_s[b], jnp.concatenate([dw.astype(BF), df], axis=1))
        wu = jnp.concatenate([w_s[b], u_s[b]], axis=1)
        dl = jnp.where(strict, -dot_nt(dx.astype(BF), wu), 0.0).astype(BF)
        d_scaled = dx[:, :HD] + dot_nn(dl, k_low)
        d_vb = dx[:, HD:]
        beta_rows = beta[rows_of(b), :]
        beta_c = stack_column(beta_rows, heads)

        windows, mixed, sigs, acts = [], [], [], []
        for c in range(3):
            window = raw_window(raw, rim, c, b)
            taps_c = conv_w[c]
            m = taps_c[0:1] * shifted(window, 0, taps)
            for j in range(1, taps):
                m = m + taps_c[j : j + 1] * shifted(window, j, taps)
            s = sigmoid(m)
            windows.append(window)
            mixed.append(m)
            sigs.append(s)
            acts.append(stack_heads(m * s, heads))
        qa, ka, va = acts
        q_scale = lax.rsqrt(jnp.sum(qa * qa, axis=1, keepdims=True) + 1e-06)
        k_scale = lax.rsqrt(jnp.sum(ka * ka, axis=1, keepdims=True) + 1e-06)
        q_unit = qa * q_scale
        k = ka * k_scale
        dk = dk + dot_tn(dl, (k * beta_c).astype(BF)) + beta_c * d_scaled
        d_beta_c = jnp.sum(d_scaled * k + d_vb * va, axis=1, keepdims=True)
        d_beta_c = jnp.broadcast_to(d_beta_c, (heads * SPAN, HD)) * beta_c * (1.0 - beta_c)
        d_beta_rows = jnp.zeros((SPAN, HD), F32)
        for h in range(heads):
            d_beta_rows = jnp.where(lane == h, d_beta_c[h * SPAN : (h + 1) * SPAN], d_beta_rows)
        d_beta[rows_of(b), :] = d_beta_rows.astype(BF)
        dq = dq * HD ** (-0.5)
        d_acts = (
            q_scale * (dq - q_unit * jnp.sum(dq * q_unit, axis=1, keepdims=True)),
            k_scale * (dk - k * jnp.sum(dk * k, axis=1, keepdims=True)),
            d_vb * beta_c,
        )
        for c in range(3):
            s, m = sigs[c], mixed[c]
            dm = spread_heads(d_acts[c], heads) * (s * (1.0 + m * (1.0 - s)))
            d_mixed[c, rows_of(b), :] = dm
            for j in range(taps):
                conv_acc[c, j] += jnp.sum((dm * shifted(windows[c], j, taps)).reshape(SPAN // 8, 8, -1), axis=0)
        return carry

    lax.fori_loop(0, blocks, grad_block, 0)
    if runs > 1:
        @pl.when(idx > 0)
        def _():
            send_to(d_mixed.at[:, pl.ds(0, 8), :], edge_in, edge_sems.at[0], edge_sems.at[1], "seq", idx - 1).start()

    for c in range(3):
        for j in range(taps):
            g_conv[c, pl.ds(j, 1), :] = jnp.sum(conv_acc[c, j], axis=0, keepdims=True)
    g_gain[...] = gain_acc[...]

    @pl.when(idx == runs - 1)
    def _():
        d_mixed[:, pl.ds(count_rows, 8), :] = jnp.zeros((3, 8, d_mixed.shape[2]), F32)

    if runs > 1:
        @pl.when(idx < runs - 1)
        def _():
            send_to(edge_in, edge_in, edge_sems.at[0], edge_sems.at[1], "seq", idx + 1).wait_recv()
            d_mixed[:, pl.ds(count_rows, 8), :] = edge_in[...]

    def raw_block(b, carry):
        for c in range(3):
            window = d_mixed[c, rows_of(b, SPAN + 8), :]
            taps_c = conv_w[c]
            total = taps_c[taps - 1 : taps] * window[:SPAN]
            for j in range(taps - 1):
                ahead = taps - 1 - j
                total = total + taps_c[j : j + 1] * window[ahead : ahead + SPAN]
            d_raw[c, rows_of(b), :] = total.astype(BF)
        return carry

    lax.fori_loop(0, blocks, raw_block, 0)
    if runs > 1:
        @pl.when(idx > 0)
        def _():
            send_to(state, state_in, state_sems.at[0], state_sems.at[1], "seq", idx - 1).wait_send()
            send_to(d_mixed.at[:, pl.ds(0, 8), :], edge_in, edge_sems.at[0], edge_sems.at[1], "seq", idx - 1).wait_send()


def delta_backward(raw, conv_w, beta, gate, gain, saved, d_gated, runs):
    count_rows, heads = beta.shape
    blocks = count_rows // SPAN
    side = heads * SPAN
    width = heads * HD
    taps = conv_w.shape[1]
    sd = jax.ShapeDtypeStruct
    q_s, k_s, w_s, u_s, t_s, p_s, f_s, s_s, o_s, rim = saved
    outs = [
        sd((3, count_rows, width), BF),
        sd((count_rows, width), BF),
        sd((count_rows, HD), BF),
        sd((3, taps, width), F32),
        sd((8, HD), F32),
    ]
    vmem = pl.BlockSpec(memory_space=pltpu.VMEM)
    return pl.pallas_call(
        functools.partial(delta_backward_kernel, heads, runs),
        out_shape=outs,
        in_specs=[vmem] * 16,
        out_specs=[vmem] * len(outs),
        scratch_shapes=[
            pltpu.VMEM((3, count_rows + 8, width), F32),
            pltpu.VMEM((blocks, side, HD), BF),
            pltpu.VMEM((blocks, side, HD), BF),
            pltpu.VMEM((blocks, side, HD), F32),
            pltpu.VMEM((blocks, heads, HD, HD), F32),
            pltpu.VMEM((blocks, heads, HD, HD), BF),
            pltpu.VMEM((heads, HD, HD), F32),
            pltpu.VMEM((heads, HD, HD), F32),
            pltpu.VMEM((3, 8, width), F32),
            pltpu.VMEM((3, taps, 8, width), F32),
            pltpu.VMEM((8, HD), F32),
            pltpu.SemaphoreType.DMA((2,)),
            pltpu.SemaphoreType.DMA((2,)),
        ],
        compiler_params=pltpu.CompilerParams(
            collective_id=1 if runs > 1 else None, has_side_effects=True, vmem_limit_bytes=56 << 20
        ),
        name="delta_backward",
    )(raw, rim, conv_w, beta, gate, gain.reshape(1, HD), q_s, k_s, w_s, u_s, t_s, p_s, f_s, s_s, o_s, d_gated)


def inverse_rms(values):
    return lax.rsqrt(jnp.mean(values * values, axis=-1, keepdims=True) + 1e-06)


def dot32(spec, a, b):
    return jnp.einsum(spec, a, b, preferred_element_type=F32)


def norm_back(values, gain, d_values):
    r = inverse_rms(values)
    e = d_values * gain
    grad_gain = jnp.sum(d_values * (values * r), axis=0)
    return r * (e - values * (r * r) * jnp.mean(e * values, axis=-1, keepdims=True)), grad_gain


def per_device(
    tokens, attn_gain, w_qkvg, w_beta, conv_w, out_gain, w_o, mlp_gain, w_gateup, w_down, cotangent
):
    runs = lax.axis_size("seq")
    everyone = ("dp", "seq")
    tok_rows = tokens[0].astype(F32)
    heads = w_beta.shape[1]
    normed = (tok_rows * inverse_rms(tok_rows) * attn_gain).astype(BF)
    projected = dot32("td,cde->cte", normed, w_qkvg)
    raw = projected[:3].astype(BF)
    gate = projected[3]
    beta = jax.nn.sigmoid(dot32("td,dh->th", normed, w_beta))
    gated, *saved = delta_forward(raw, conv_w, beta, gate, out_gain, runs)
    norm_part = saved.pop()[0, 0]
    attn = lax.psum(dot32("tc,cd->td", gated, w_o).astype(BF), "head").astype(F32)
    hidden = tok_rows + attn
    normed_mlp = (hidden * inverse_rms(hidden) * mlp_gain).astype(BF)
    gate_up = dot32("td,cdf->ctf", normed_mlp, w_gateup)
    gate_act, up_act = gate_up[0], gate_up[1]
    sig = jax.nn.sigmoid(gate_act)
    silu = gate_act * sig
    units = (silu * up_act).astype(BF)
    mlp_out = lax.psum(dot32("tf,fd->td", units, w_down).astype(BF), "head").astype(F32)
    result = (hidden + mlp_out).astype(BF)
    cot = cotangent[0]
    d_hidden = dot32("td,fd->tf", cot, w_down)
    d_gate_up = jnp.stack(
        [d_hidden * up_act * (sig + silu * (1.0 - sig)), d_hidden * silu], axis=0
    ).astype(BF)
    d_normed_mlp = lax.psum(dot32("ctf,cdf->td", d_gate_up, w_gateup).astype(BF), "head").astype(F32)
    d_hidden_part, grad_mlp_gain = norm_back(hidden, mlp_gain, d_normed_mlp)
    d_hidden_state = cot.astype(F32) + d_hidden_part
    d_attn = d_hidden_state.astype(BF)
    d_gated = dot32("td,cd->tc", d_attn, w_o)
    d_raw, d_gate, d_beta, grad_conv, grad_gain_rows = delta_backward(
        raw, conv_w, beta, gate, out_gain, saved, d_gated, runs
    )
    d_beta = d_beta[:, :heads]
    d_proj = jnp.concatenate([d_raw, d_gate[None]], axis=0)
    d_normed = lax.psum(
        (dot32("cte,cde->td", d_proj, w_qkvg) + dot32("th,dh->td", d_beta, w_beta)).astype(BF), "head"
    ).astype(F32)
    d_tok_part, grad_attn_gain = norm_back(tok_rows, attn_gain, d_normed)
    d_tokens = (d_hidden_state + d_tok_part).astype(BF)
    grad_down = dot32("tf,td->fd", units, cot).astype(BF)
    grad_gateup = dot32("td,ctf->cdf", normed_mlp, d_gate_up).astype(BF)
    grad_o = dot32("tc,td->cd", gated, d_attn).astype(BF)
    grad_qkvg = dot32("td,cte->cde", normed, d_proj).astype(BF)
    grad_beta = dot32("td,th->dh", normed, d_beta)
    out_gain_head, norm_head = lax.psum((jnp.sum(grad_gain_rows, axis=0), norm_part), "head")
    small = lax.psum(
        (grad_attn_gain, grad_mlp_gain, out_gain_head, grad_conv, grad_beta, norm_head), everyone
    )
    sum_gateup = lax.psum_scatter(grad_gateup, everyone, scatter_dimension=1, tiled=True).astype(F32)
    sum_down = lax.psum_scatter(grad_down, everyone, scatter_dimension=1, tiled=True).astype(F32)
    sum_o = lax.psum_scatter(grad_o, everyone, scatter_dimension=1, tiled=True).astype(F32)
    sum_qkvg = lax.psum_scatter(grad_qkvg, everyone, scatter_dimension=1, tiled=True).astype(F32)
    state_mean = small[5] / (lax.axis_size("dp") * runs * heads * lax.axis_size("head"))
    return (
        result[None],
        d_tokens[None],
        small[0],
        sum_qkvg,
        small[4],
        small[3],
        small[2],
        sum_o,
        small[1],
        sum_gateup,
        sum_down,
        state_mean,
    )


def solution(mesh):
    rows, halves_of = P("dp", "seq", None), P(None, None, "head")
    placed = (
        rows, P(), halves_of, P(None, "head"), halves_of, P(), P("head", None), P(),
        halves_of, P("head", None), rows,
    )
    shared = P(None, ("dp", "seq"), "head")
    turned = P("head", ("dp", "seq"))
    return jax.shard_map(
        per_device,
        mesh=mesh,
        in_specs=placed,
        out_specs=(
            rows, rows, P(), shared, P(None, "head"), halves_of, P(), turned, P(), shared, turned, P(),
        ),
        check_vma=False,
    )
```

```python
import functools

import jax
import jax.numpy as jnp
from jax import lax
from jax.experimental import pallas as pl
from jax.experimental.pallas import tpu as pltpu
from jax.sharding import PartitionSpec as P

HD = 128
SPAN = 64
RIM = 16
PIECE = 32


MESH_ID = pl.DeviceIdType.MESH
F32 = jnp.float32
BF = jnp.bfloat16


def dot_nn(a, b):
    return lax.dot_general(a, b, (((1,), (0,)), ((), ())), preferred_element_type=F32)


def dot_nt(a, b):
    return lax.dot_general(a, b, (((1,), (1,)), ((), ())), preferred_element_type=F32)


def dot_tn(a, b):
    return lax.dot_general(a, b, (((0,), (0,)), ((), ())), preferred_element_type=F32)


def halves(a):
    high = a.astype(BF)
    return high, (a - high.astype(F32)).astype(BF)


def dot_fine(a, b, dot=dot_nn):
    a_high, a_rest = halves(a)
    b_high, b_rest = halves(b)
    return dot(a_high, b_high) + (dot(a_high, b_rest) + dot(a_rest, b_high))


def stack_heads(x, heads):
    return jnp.concatenate([x[:, h * HD : (h + 1) * HD] for h in range(heads)], axis=0)


def spread_heads(x, heads):
    return jnp.concatenate([x[h * SPAN : (h + 1) * SPAN] for h in range(heads)], axis=1)


def stack_column(x, heads):
    return jnp.concatenate(
        [jnp.broadcast_to(x[:, h : h + 1], (SPAN, HD)) for h in range(heads)], axis=0
    )


def sigmoid(x):
    return 1.0 / (1.0 + jnp.exp(-x))


def rows_of(b, count=SPAN):
    return pl.ds(pl.multiple_of(b * SPAN, SPAN), count)


def raw_window(raw, rim, c, b):
    now = raw[c, rows_of(b), :].astype(F32)
    start = pl.multiple_of(jnp.maximum(b * SPAN - RIM, 0), RIM)
    before = jnp.where(b == 0, rim[c].astype(F32), raw[c, pl.ds(start, RIM), :].astype(F32))
    return jnp.concatenate([before[RIM - 8 :], now], axis=0)


def shifted(window, j, taps):
    start = 8 - (taps - 1) + j
    return window[start : start + SPAN]


def meet(idx, count, axis):
    barrier = pltpu.get_barrier_semaphore()

    @pl.when(idx > 0)
    def _():
        pl.semaphore_signal(barrier, inc=1, device_id={axis: idx - 1}, device_id_type=MESH_ID)

    @pl.when(idx < count - 1)
    def _():
        pl.semaphore_signal(barrier, inc=1, device_id={axis: idx + 1}, device_id_type=MESH_ID)

    ends = (idx == 0) | (idx == count - 1)

    @pl.when(ends)
    def _():
        pl.semaphore_wait(barrier, 1)

    if count > 2:
        @pl.when(jnp.logical_not(ends))
        def _():
            pl.semaphore_wait(barrier, 2)


def send_to(src, dst, send_sem, recv_sem, axis, target):
    return pltpu.make_async_remote_copy(
        src_ref=src,
        dst_ref=dst,
        send_sem=send_sem,
        recv_sem=recv_sem,
        device_id={axis: target},
        device_id_type=MESH_ID,
    )


def block_masks(heads):
    side = heads * SPAN
    row = lax.broadcasted_iota(jnp.int32, (side, side), 0)
    col = lax.broadcasted_iota(jnp.int32, (side, side), 1)
    same = (row // SPAN) == (col // SPAN)
    return row, col, same & (row > col), same & (row >= col)


def unit_lower_inverse(lower, row, col):
    inverse = jnp.where(row == col, 1.0, 0.0) - jnp.where((row // 2) == (col // 2), lower, 0.0)
    m = 2
    while m < SPAN:
        off = jnp.where(((row // (2 * m)) == (col // (2 * m))) & ((row // m) != (col // m)), lower, 0.0)
        inverse = inverse - dot_fine(dot_fine(inverse, off), inverse)
        m *= 2
    return inverse


def delta_forward_kernel(
    heads, runs, raw, conv_w, beta, gate, gain,
    gated, q_s, k_s, w_s, u_s, t_s, p_s, f_s, s_s, o_s, rim, norm,
    u_full, state, state_in, rim_in, rim_sems, state_sems,
):
    idx = lax.axis_index("seq")
    count_rows = raw.shape[1]
    taps = conv_w.shape[1]
    blocks = count_rows // SPAN
    last = count_rows - RIM
    if runs > 1:
        meet(idx, runs, "seq")

        @pl.when(idx < runs - 1)
        def _():
            send_to(raw.at[:, pl.ds(last, RIM), :], rim_in, rim_sems.at[0], rim_sems.at[1], "seq", idx + 1).start()

    row, col, strict, causal = block_masks(heads)

    def prepare_group(g, group):
        @pl.when(g == 0)
        def _():
            @pl.when(idx == 0)
            def _():
                rim[...] = jnp.zeros_like(rim)

            if runs > 1:
                @pl.when(idx > 0)
                def _():
                    send_to(rim_in, rim_in, rim_sems.at[0], rim_sems.at[1], "seq", idx - 1).wait_recv()
                    rim[...] = rim_in[...]

        for part in range(group):
            b = g * group + part
            parts = []
            for c in range(3):
                window = raw_window(raw, rim, c, b)
                taps_c = conv_w[c]
                mixed = taps_c[0:1] * shifted(window, 0, taps)
                for j in range(1, taps):
                    mixed = mixed + taps_c[j : j + 1] * shifted(window, j, taps)
                parts.append(stack_heads(mixed * sigmoid(mixed), heads))
            q, k, v = parts
            q = q * (lax.rsqrt(jnp.sum(q * q, axis=1, keepdims=True) + 1e-06) * HD ** (-0.5))
            k = k * lax.rsqrt(jnp.sum(k * k, axis=1, keepdims=True) + 1e-06)
            beta_c = stack_column(beta[rows_of(b), :], heads)
            scaled = k * beta_c
            lower = jnp.where(strict, dot_fine(scaled, k, dot_nt), 0.0)
            inverse = unit_lower_inverse(lower, row, col).astype(BF)
            k_low = k.astype(BF)
            q_low = q.astype(BF)
            wu = dot_nn(inverse, jnp.concatenate([scaled, v * beta_c], axis=1).astype(BF))
            attention = jnp.where(causal, dot_nt(q_low, k_low), 0.0)
            q_s[b] = q_low
            k_s[b] = k_low
            t_s[b] = inverse
            p_s[b] = attention.astype(BF)
            w_s[b] = wu[:, :HD].astype(BF)
            u_full[b] = wu[:, HD:]
            u_s[b] = wu[:, HD:].astype(BF)

    group = 2
    groups = blocks // group

    def prepare_loop(i, carry):
        prepare_group(groups - 1 - i, group)
        return carry

    lax.fori_loop(0, groups, prepare_loop, 0)

    @pl.when(idx == 0)
    def _():
        state[...] = jnp.zeros_like(state)

    if runs > 1:
        @pl.when(idx > 0)
        def _():
            send_to(state_in, state_in, state_sems.at[0], state_sems.at[1], "seq", idx - 1).wait_recv()
            state[...] = state_in[...]

    gain_row = gain[...]

    def scan_block(b, carry):
        fresh, out_part = [], []
        before = [state[h] for h in range(heads)]
        for h in range(heads):
            mine = pl.ds(h * SPAN, SPAN)
            low = before[h].astype(BF)
            s_s[b, h] = low
            both = dot_nn(jnp.concatenate([w_s[b, mine, :], q_s[b, mine, :]], axis=0), low)
            fresh.append(u_full[b, mine, :] - both[:SPAN])
            out_part.append(both[SPAN:])
        for h in range(heads):
            mine = pl.ds(h * SPAN, SPAN)
            state[h] = before[h] + dot_tn(k_s[b, mine, :], fresh[h].astype(BF))
        fresh_low = jnp.concatenate(fresh, axis=0).astype(BF)
        f_s[b] = fresh_low
        out = jnp.concatenate(out_part, axis=0) + dot_nn(p_s[b], fresh_low)
        o_s[b] = out
        g = stack_heads(gate[rows_of(b), :], heads)
        scale = lax.rsqrt(jnp.mean(out * out, axis=1, keepdims=True) + 1e-05)
        gated[rows_of(b), :] = spread_heads(out * scale * gain_row * (g * sigmoid(g)), heads).astype(BF)
        return carry

    lax.fori_loop(0, blocks, scan_block, 0)
    if runs > 1:
        @pl.when(idx < runs - 1)
        def _():
            send_to(state, state_in, state_sems.at[0], state_sems.at[1], "seq", idx + 1).start()

    total = jnp.zeros((1, HD), F32)
    for h in range(heads):
        end = state[h]
        square = jnp.sum(jnp.sum(end * end, axis=0, keepdims=True), axis=1, keepdims=True)
        total = total + jnp.broadcast_to(jnp.sqrt(square), (1, HD))
    norm[...] = jnp.broadcast_to(total, norm.shape)
    if runs > 1:
        @pl.when(idx < runs - 1)
        def _():
            send_to(raw.at[:, pl.ds(last, RIM), :], rim_in, rim_sems.at[0], rim_sems.at[1], "seq", idx + 1).wait_send()
            send_to(state, state_in, state_sems.at[0], state_sems.at[1], "seq", idx + 1).wait_send()


def delta_forward(raw, conv_w, beta, gate, gain, runs):
    count_rows, heads = beta.shape
    blocks = count_rows // SPAN
    side = heads * SPAN
    width = heads * HD
    sd = jax.ShapeDtypeStruct
    outs = [
        sd((count_rows, width), BF),
        sd((blocks, side, HD), BF),
        sd((blocks, side, HD), BF),
        sd((blocks, side, HD), BF),
        sd((blocks, side, HD), BF),
        sd((blocks, side, side), BF),
        sd((blocks, side, side), BF),
        sd((blocks, side, HD), BF),
        sd((blocks, heads, HD, HD), BF),
        sd((blocks, side, HD), F32),
        sd((3, RIM, width), BF),
        sd((8, HD), F32),
    ]
    vmem = pl.BlockSpec(memory_space=pltpu.VMEM)
    return pl.pallas_call(
        functools.partial(delta_forward_kernel, heads, runs),
        out_shape=outs,
        in_specs=[vmem] * 5,
        out_specs=[vmem] * len(outs),
        scratch_shapes=[
            pltpu.VMEM((blocks, side, HD), F32),
            pltpu.VMEM((heads, HD, HD), F32),
            pltpu.VMEM((heads, HD, HD), F32),
            pltpu.VMEM((3, RIM, width), BF),
            pltpu.SemaphoreType.DMA((2,)),
            pltpu.SemaphoreType.DMA((2,)),
        ],
        compiler_params=pltpu.CompilerParams(
            collective_id=0 if runs > 1 else None, has_side_effects=True, vmem_limit_bytes=48 << 20
        ),
        cost_estimate=pl.CostEstimate(flops=0, transcendentals=0, bytes_accessed=count_rows * width * 400),
        name="delta_forward",
    )(raw, conv_w, beta, gate, gain.reshape(1, HD))


def delta_backward_kernel(
    heads, runs, raw, rim, conv_w, beta, gate, gain,
    q_s, k_s, w_s, u_s, t_s, p_s, f_s, s_s, o_s, d_gated,
    d_raw, d_gate, d_beta, g_conv, g_gain,
    d_mixed, d_out, d_fresh, d_fresh0, q_out, after_s, state, state_in, edge_in, conv_acc, gain_acc,
    state_sems, edge_sems,
):
    idx = lax.axis_index("seq")
    count_rows = raw.shape[1]
    taps = conv_w.shape[1]
    blocks = count_rows // SPAN
    if runs > 1:
        meet(idx, runs, "seq")
    gain_row = gain[...]
    gain_acc[...] = jnp.zeros_like(gain_acc)
    conv_acc[...] = jnp.zeros_like(conv_acc)

    def gate_block(b, carry):
        o = o_s[b]
        g = stack_heads(gate[rows_of(b), :], heads)
        dg = stack_heads(d_gated[rows_of(b), :].astype(F32), heads)
        scale = lax.rsqrt(jnp.mean(o * o, axis=1, keepdims=True) + 1e-05)
        y = o * scale
        sig = sigmoid(g)
        silu = g * sig
        dgy = dg * y
        gain_acc[...] += jnp.sum((dgy * silu).reshape(-1, 8, HD), axis=0)
        d_gate[rows_of(b), :] = spread_heads(dgy * gain_row * (sig + silu * (1.0 - sig)), heads).astype(BF)
        dy = dg * gain_row * silu
        do = (scale * (dy - y * jnp.mean(dy * y, axis=1, keepdims=True))).astype(BF)
        d_out[b] = do
        d_fresh0[b] = dot_tn(p_s[b], do)
        for h in range(heads):
            mine = slice(h * SPAN, (h + 1) * SPAN)
            q_out[b, h] = dot_tn(q_s[b, mine, :], do[mine])
        return carry

    lax.fori_loop(0, blocks, gate_block, 0)

    @pl.when(idx == runs - 1)
    def _():
        state[...] = jnp.zeros_like(state)

    if runs > 1:
        @pl.when(idx < runs - 1)
        def _():
            send_to(state_in, state_in, state_sems.at[0], state_sems.at[1], "seq", idx + 1).wait_recv()
            state[...] = state_in[...]

    def scan_block(i, carry):
        b = blocks - 1 - i
        for h in range(heads):
            mine = pl.ds(h * SPAN, SPAN)
            after = state[h]
            low = after.astype(BF)
            after_s[b, h] = low
            df = (d_fresh0[b, mine, :] + dot_nn(k_s[b, mine, :], low)).astype(BF)
            d_fresh[b, mine, :] = df
            state[h] = after + q_out[b, h] - dot_tn(w_s[b, mine, :], df)
        return carry

    lax.fori_loop(0, blocks, scan_block, 0)
    if runs > 1:
        @pl.when(idx > 0)
        def _():
            send_to(state, state_in, state_sems.at[0], state_sems.at[1], "seq", idx - 1).start()

    row, col, strict, causal = block_masks(heads)
    lane = lax.broadcasted_iota(jnp.int32, (SPAN, HD), 1)

    def grad_block(b, carry):
        df = d_fresh[b]
        do = d_out[b]
        k_low = k_s[b]
        dw, dq, dk = [], [], []
        for h in range(heads):
            mine = slice(h * SPAN, (h + 1) * SPAN)
            both = dot_nt(jnp.concatenate([df[mine], do[mine]], axis=0), s_s[b, h])
            dw.append(-both[:SPAN])
            dq.append(both[SPAN:])
            dk.append(dot_nt(f_s[b, mine, :], after_s[b, h]))
        dw = jnp.concatenate(dw, axis=0)
        dp = jnp.where(causal, dot_nt(do, f_s[b]), 0.0).astype(BF)
        dq = jnp.concatenate(dq, axis=0) + dot_nn(dp, k_low)
        dk = jnp.concatenate(dk, axis=0) + dot_tn(dp, q_s[b])
        dx = dot_tn(t_s[b], jnp.concatenate([dw.astype(BF), df], axis=1))
        wu = jnp.concatenate([w_s[b], u_s[b]], axis=1)
        dl = jnp.where(strict, -dot_nt(dx.astype(BF), wu), 0.0).astype(BF)
        d_scaled = dx[:, :HD] + dot_nn(dl, k_low)
        d_vb = dx[:, HD:]
        beta_rows = beta[rows_of(b), :]
        beta_c = stack_column(beta_rows, heads)

        windows, mixed, sigs, acts = [], [], [], []
        for c in range(3):
            window = raw_window(raw, rim, c, b)
            taps_c = conv_w[c]
            m = taps_c[0:1] * shifted(window, 0, taps)
            for j in range(1, taps):
                m = m + taps_c[j : j + 1] * shifted(window, j, taps)
            s = sigmoid(m)
            windows.append(window)
            mixed.append(m)
            sigs.append(s)
            acts.append(stack_heads(m * s, heads))
        qa, ka, va = acts
        q_scale = lax.rsqrt(jnp.sum(qa * qa, axis=1, keepdims=True) + 1e-06)
        k_scale = lax.rsqrt(jnp.sum(ka * ka, axis=1, keepdims=True) + 1e-06)
        q_unit = qa * q_scale
        k = ka * k_scale
        dk = dk + dot_tn(dl, (k * beta_c).astype(BF)) + beta_c * d_scaled
        d_beta_c = jnp.sum(d_scaled * k + d_vb * va, axis=1, keepdims=True)
        d_beta_c = jnp.broadcast_to(d_beta_c, (heads * SPAN, HD)) * beta_c * (1.0 - beta_c)
        d_beta_rows = jnp.zeros((SPAN, HD), F32)
        for h in range(heads):
            d_beta_rows = jnp.where(lane == h, d_beta_c[h * SPAN : (h + 1) * SPAN], d_beta_rows)
        d_beta[rows_of(b), :] = d_beta_rows.astype(BF)
        dq = dq * HD ** (-0.5)
        d_acts = (
            q_scale * (dq - q_unit * jnp.sum(dq * q_unit, axis=1, keepdims=True)),
            k_scale * (dk - k * jnp.sum(dk * k, axis=1, keepdims=True)),
            d_vb * beta_c,
        )
        for c in range(3):
            s, m = sigs[c], mixed[c]
            dm = spread_heads(d_acts[c], heads) * (s * (1.0 + m * (1.0 - s)))
            d_mixed[c, rows_of(b), :] = dm
            for j in range(taps):
                conv_acc[c, j] += jnp.sum((dm * shifted(windows[c], j, taps)).reshape(SPAN // 8, 8, -1), axis=0)
        return carry

    lax.fori_loop(0, blocks, grad_block, 0)
    if runs > 1:
        @pl.when(idx > 0)
        def _():
            send_to(d_mixed.at[:, pl.ds(0, 8), :], edge_in, edge_sems.at[0], edge_sems.at[1], "seq", idx - 1).start()

    for c in range(3):
        for j in range(taps):
            g_conv[c, pl.ds(j, 1), :] = jnp.sum(conv_acc[c, j], axis=0, keepdims=True)
    g_gain[...] = gain_acc[...]

    @pl.when(idx == runs - 1)
    def _():
        d_mixed[:, pl.ds(count_rows, 8), :] = jnp.zeros((3, 8, d_mixed.shape[2]), F32)

    if runs > 1:
        @pl.when(idx < runs - 1)
        def _():
            send_to(edge_in, edge_in, edge_sems.at[0], edge_sems.at[1], "seq", idx + 1).wait_recv()
            d_mixed[:, pl.ds(count_rows, 8), :] = edge_in[...]

    def raw_block(b, carry):
        for c in range(3):
            window = d_mixed[c, rows_of(b, SPAN + 8), :]
            taps_c = conv_w[c]
            total = taps_c[taps - 1 : taps] * window[:SPAN]
            for j in range(taps - 1):
                ahead = taps - 1 - j
                total = total + taps_c[j : j + 1] * window[ahead : ahead + SPAN]
            d_raw[c, rows_of(b), :] = total.astype(BF)
        return carry

    lax.fori_loop(0, blocks, raw_block, 0)
    if runs > 1:
        @pl.when(idx > 0)
        def _():
            send_to(state, state_in, state_sems.at[0], state_sems.at[1], "seq", idx - 1).wait_send()
            send_to(d_mixed.at[:, pl.ds(0, 8), :], edge_in, edge_sems.at[0], edge_sems.at[1], "seq", idx - 1).wait_send()


def delta_backward(raw, conv_w, beta, gate, gain, saved, d_gated, runs):
    count_rows, heads = beta.shape
    blocks = count_rows // SPAN
    side = heads * SPAN
    width = heads * HD
    taps = conv_w.shape[1]
    sd = jax.ShapeDtypeStruct
    q_s, k_s, w_s, u_s, t_s, p_s, f_s, s_s, o_s, rim = saved
    outs = [
        sd((3, count_rows, width), BF),
        sd((count_rows, width), BF),
        sd((count_rows, HD), BF),
        sd((3, taps, width), F32),
        sd((8, HD), F32),
    ]
    vmem = pl.BlockSpec(memory_space=pltpu.VMEM)
    return pl.pallas_call(
        functools.partial(delta_backward_kernel, heads, runs),
        out_shape=outs,
        in_specs=[vmem] * 16,
        out_specs=[vmem] * len(outs),
        scratch_shapes=[
            pltpu.VMEM((3, count_rows + 8, width), F32),
            pltpu.VMEM((blocks, side, HD), BF),
            pltpu.VMEM((blocks, side, HD), BF),
            pltpu.VMEM((blocks, side, HD), F32),
            pltpu.VMEM((blocks, heads, HD, HD), F32),
            pltpu.VMEM((blocks, heads, HD, HD), BF),
            pltpu.VMEM((heads, HD, HD), F32),
            pltpu.VMEM((heads, HD, HD), F32),
            pltpu.VMEM((3, 8, width), F32),
            pltpu.VMEM((3, taps, 8, width), F32),
            pltpu.VMEM((8, HD), F32),
            pltpu.SemaphoreType.DMA((2,)),
            pltpu.SemaphoreType.DMA((2,)),
        ],
        compiler_params=pltpu.CompilerParams(
            collective_id=1 if runs > 1 else None, has_side_effects=True, vmem_limit_bytes=56 << 20
        ),
        cost_estimate=pl.CostEstimate(flops=0, transcendentals=0, bytes_accessed=count_rows * width * 400),
        name="delta_backward",
    )(raw, rim, conv_w, beta, gate, gain.reshape(1, HD), q_s, k_s, w_s, u_s, t_s, p_s, f_s, s_s, o_s, d_gated)


def plan_head_sum(size, subs, count):
    tasks = {}
    for g in range(count):
        for s in range(subs):
            for m in range(size):
                for q in range(size - 1):
                    tasks[(0, m, g, s, q)] = None
                    tasks[(1, m, g, s, q + 1)] = None
    done = {}

    def ready(task):
        way, m, g, s, q = task
        j = size - 1 - m if way == 0 else m
        back = q - 1 if way == 0 else q + 1
        needs = []
        if 0 <= back < size:
            needs.append((way, m, g, s, back))
        if j == q:
            other = q + 1 if way == 0 else q - 1
            if 0 <= other < size:
                needs.append((1 - way, q if way == 0 else size - 1 - q, g, s, other))
        times = [done.get(n) for n in needs]
        if any(t is None for t in times):
            return None
        return max([0.0] + times)

    free = {}
    order = {p: [] for p in range(size)}
    pending = set(tasks)
    while pending:
        best = None
        for task in pending:
            at = ready(task)
            if at is None:
                continue
            link = (task[0], task[4])
            start = max(at, free.get(link, 0.0))
            key = (start, task[1], task[2], task[3], task[0], task[4])
            if best is None or key < best[0]:
                best = (key, task)
        (start, *_), task = best
        pending.remove(task)
        free[(task[0], task[4])] = start + 1.0
        done[task] = start + 1.0 + 0.5
        order[task[4]].append(task[:4])
    return order


def head_sum_body(size, subs, parts, arrive, outs, finish, send_sems, recv_sems):
    count = len(parts)
    idx = lax.axis_index("head")
    rows = parts[0].shape[0] // size
    sub = rows // subs
    orders = plan_head_sum(size, subs, count)
    meet(idx, size, "head")

    def at(j, s):
        return pl.ds(j * rows + s * sub, sub)

    def device(p):
        waited, finals = set(), set()

        def copy(way, m, g, s, to=None):
            j = size - 1 - m if way == 0 else m
            sender = p if to is not None else (p - 1 if way == 0 else p + 1)
            summing = sender < j if way == 0 else sender > j
            upstream = sender > 0 if way == 0 else sender < size - 1
            dst = arrive[g][way] if summing else outs[g]
            src = (arrive[g][way] if upstream else parts[g]) if summing else outs[g]
            if to is None:
                src = dst
            n = ((g * subs + s) * 2 + way) * size + m
            return pltpu.make_async_remote_copy(
                src_ref=src.at[at(j, s), :],
                dst_ref=dst.at[at(j, s), :],
                send_sem=send_sems.at[n],
                recv_sem=recv_sems.at[n],
                device_id={"head": (p + 1 if way == 0 else p - 1) if to is not None else sender},
                device_id_type=MESH_ID,
            )

        def has_upstream(way):
            return p > 0 if way == 0 else p < size - 1

        def need(way, m, g, s):
            if has_upstream(way) and (way, m, g, s) not in waited:
                copy(way, m, g, s).wait_recv()
                waited.add((way, m, g, s))

        for way, m, g, s in orders[p]:
            j = size - 1 - m if way == 0 else m
            if j == p:
                if (g, s) not in finals:
                    finals.add((g, s))
                    need(0, size - 1 - p, g, s)
                    need(1, p, g, s)
                    sides = [arrive[g][w] for w in range(2) if has_upstream(w)]
                    finish(g, p, s, sides)
            else:
                need(way, m, g, s)
                summing = p < j if way == 0 else p > j
                if summing and has_upstream(way):
                    box = arrive[g][way]

                    def add(i, carry, box=box, g=g, j=j, s=s):
                        r = pl.ds(pl.multiple_of(j * rows + s * sub + i * 16, 16), 16)
                        box[r, :] = (box[r, :].astype(F32) + parts[g][r, :].astype(F32)).astype(BF)
                        return carry

                    lax.fori_loop(0, sub // 16, add, 0)
            copy(way, m, g, s, to=True).start()
        for g in range(count):
            for s in range(subs):
                for way in range(2):
                    for m in range(size):
                        need(way, m, g, s)
        for way, m, g, s in orders[p]:
            copy(way, m, g, s, to=True).wait_send()

    for p in range(size):
        pl.when(idx == p)(functools.partial(device, p))


def own_rows(p, s, i, rows, sub):
    start = s * sub + i * 16
    return (
        pl.ds(pl.multiple_of(p * rows + start, 16), 16),
        pl.ds(pl.multiple_of(start, 16), 16),
    )


def total_rows(part, sides, r):
    total = part[r, :].astype(F32)
    for side in sides:
        total = total + side[r, :].astype(F32)
    return total


def norm_back_rows(x, gain, d):
    r = lax.rsqrt(jnp.mean(x * x, axis=1, keepdims=True) + 1e-06)
    e = d * gain
    unit = x * r
    gain_part = d * unit
    return r * (e - unit * jnp.mean(e * unit, axis=1, keepdims=True)), gain_part


def mixer_sum_kernel(size, subs, part, tokens, gain, hidden, normed, right, left, send_sems, recv_sems):
    rows = part.shape[0] // size
    sub = rows // subs

    def finish(g, p, s, sides):
        def step(i, carry):
            r, own = own_rows(p, s, i, rows, sub)
            x = tokens[r, :].astype(F32) + total_rows(part, sides, r)
            hidden[own, :] = x
            scale = lax.rsqrt(jnp.mean(x * x, axis=1, keepdims=True) + 1e-06)
            normed[r, :] = (x * scale * gain[...]).astype(BF)
            return carry

        lax.fori_loop(0, sub // 16, step, 0)

    head_sum_body(size, subs, [part], [(right, left)], [normed], finish, send_sems, recv_sems)


def mlp_back_kernel(size, subs, part, hidden, cot, gain, d_hidden, gain_sum, d_attn, right, left, send_sems, recv_sems):
    rows = part.shape[0] // size
    sub = rows // subs
    gain_sum[...] = jnp.zeros_like(gain_sum)

    def finish(g, p, s, sides):
        def step(i, carry):
            r, own = own_rows(p, s, i, rows, sub)
            back, gain_part = norm_back_rows(hidden[own, :], gain[...], total_rows(part, sides, r))
            x = cot[r, :].astype(F32) + back
            d_hidden[own, :] = x
            d_attn[r, :] = x.astype(BF)
            gain_sum[...] += jnp.sum(gain_part.reshape(2, 8, -1), axis=0)
            return carry

        lax.fori_loop(0, sub // 16, step, 0)

    head_sum_body(size, subs, [part], [(right, left)], [d_attn], finish, send_sems, recv_sems)


def last_sum_kernel(
    size, subs, part, mlp_part, tokens, hidden, d_hidden, gain, gain_sum, d_tokens, result,
    right, left, right2, left2, send_sems, recv_sems,
):
    rows = part.shape[0] // size
    sub = rows // subs
    gain_sum[...] = jnp.zeros_like(gain_sum)

    def finish(g, p, s, sides):
        def step(i, carry):
            r, own = own_rows(p, s, i, rows, sub)
            if g == 0:
                back, gain_part = norm_back_rows(tokens[r, :].astype(F32), gain[...], total_rows(part, sides, r))
                d_tokens[r, :] = (d_hidden[own, :] + back).astype(BF)
                gain_sum[...] += jnp.sum(gain_part.reshape(2, 8, -1), axis=0)
            else:
                result[r, :] = (hidden[own, :] + total_rows(mlp_part, sides, r)).astype(BF)
            return carry

        lax.fori_loop(0, sub // 16, step, 0)

    head_sum_body(
        size, subs, [part, mlp_part], [(right, left), (right2, left2)], [d_tokens, result], finish, send_sems, recv_sems
    )


def head_sum_call(kernel, name, collective_id, size, sums, outs, *args):
    count_rows, width = args[0].shape
    subs = count_rows // size // PIECE
    vmem = pl.BlockSpec(memory_space=pltpu.VMEM)
    sems = pltpu.SemaphoreType.DMA((sums * subs * 2 * size,))
    return pl.pallas_call(
        functools.partial(kernel, size, subs),
        out_shape=outs,
        in_specs=[vmem] * len(args),
        out_specs=[vmem] * len(outs),
        scratch_shapes=[pltpu.VMEM((count_rows, width), BF)] * (2 * sums) + [sems, sems],
        compiler_params=pltpu.CompilerParams(
            collective_id=collective_id, has_side_effects=True, vmem_limit_bytes=56 << 20
        ),
        cost_estimate=pl.CostEstimate(flops=0, transcendentals=0, bytes_accessed=sums * count_rows * width * 64),
        name=name,
    )(*args)


def inverse_rms(values):
    return lax.rsqrt(jnp.mean(values * values, axis=-1, keepdims=True) + 1e-06)


def dot32(spec, a, b):
    return jnp.einsum(spec, a, b, preferred_element_type=F32)


def per_device(
    tokens, attn_gain, w_qkvg, w_beta, conv_w, out_gain, w_o, mlp_gain, w_gateup, w_down, cotangent
):
    runs = lax.axis_size("seq")
    size = lax.axis_size("head")
    everyone = ("dp", "seq")
    tokens = tokens[0]
    cot = cotangent[0]
    count_rows, width = tokens.shape
    own = count_rows // size
    sd = jax.ShapeDtypeStruct
    whole, mine, gain_rows = sd((count_rows, width), BF), sd((own, width), F32), sd((8, width), F32)
    tok_rows = tokens.astype(F32)
    heads = w_beta.shape[1]
    normed = (tok_rows * inverse_rms(tok_rows) * attn_gain).astype(BF)
    projected = dot32("td,cde->cte", normed, w_qkvg)
    raw = projected[:3].astype(BF)
    gate = projected[3]
    beta = jax.nn.sigmoid(dot32("td,dh->th", normed, w_beta))
    gated, *saved = delta_forward(raw, conv_w, beta, gate, out_gain, runs)
    norm_part = saved.pop()[0, 0]
    attn_part = dot32("tc,cd->td", gated, w_o).astype(BF)
    hidden, normed_mlp = head_sum_call(
        mixer_sum_kernel, "mixer_sum", 2, size, 1, [mine, whole], attn_part, tokens, mlp_gain.reshape(1, -1)
    )
    gate_up = dot32("td,cdf->ctf", normed_mlp, w_gateup)
    gate_act, up_act = gate_up[0], gate_up[1]
    sig = jax.nn.sigmoid(gate_act)
    silu = gate_act * sig
    units = (silu * up_act).astype(BF)
    d_hidden = dot32("td,fd->tf", cot, w_down)
    d_gate_up = jnp.stack(
        [d_hidden * up_act * (sig + silu * (1.0 - sig)), d_hidden * silu], axis=0
    ).astype(BF)
    grad_mlp = jnp.concatenate(
        [
            dot32("td,ctf->cdf", normed_mlp, d_gate_up).astype(BF),
            dot32("td,tf->df", cot, units).astype(BF)[None],
        ],
        axis=0,
    )
    mlp_back_part = dot32("ctf,cdf->td", d_gate_up, w_gateup).astype(BF)
    grad_mlp, mlp_back_part = lax.optimization_barrier((grad_mlp, mlp_back_part))
    sum_mlp = lax.psum_scatter(grad_mlp, everyone, scatter_dimension=1, tiled=True)
    d_hidden_rows, mlp_gain_rows, d_attn = head_sum_call(
        mlp_back_kernel, "mlp_back", 3, size, 1, [mine, gain_rows, whole],
        mlp_back_part, hidden, cot, mlp_gain.reshape(1, -1),
    )
    mlp_part = dot32("tf,fd->td", units, w_down).astype(BF)
    d_gated = dot32("td,cd->tc", d_attn, w_o)
    d_raw, d_gate, d_beta, grad_conv, out_gain_rows = delta_backward(
        raw, conv_w, beta, gate, out_gain, saved, d_gated, runs
    )
    d_beta = d_beta[:, :heads]
    d_proj = jnp.concatenate([d_raw, d_gate[None]], axis=0)
    d_normed_part = (dot32("cte,cde->td", d_proj, w_qkvg) + dot32("th,dh->td", d_beta, w_beta)).astype(BF)
    grad_mixer = jnp.concatenate(
        [
            dot32("td,cte->cde", normed, d_proj).astype(BF),
            dot32("td,tc->dc", d_attn, gated).astype(BF)[None],
        ],
        axis=0,
    )
    grad_beta = dot32("td,th->dh", normed, d_beta)
    grad_mixer, d_normed_part, sum_mlp = lax.optimization_barrier((grad_mixer, d_normed_part, sum_mlp))
    attn_gain_rows, d_tokens, result = head_sum_call(
        last_sum_kernel, "last_sum", 4, size, 2, [gain_rows, whole, whole],
        d_normed_part, mlp_part, tokens, hidden, d_hidden_rows, attn_gain.reshape(1, -1),
    )
    everywhere = lax.psum(
        (
            jnp.sum(attn_gain_rows, axis=0),
            jnp.sum(mlp_gain_rows, axis=0),
            jnp.sum(out_gain_rows, axis=0),
            norm_part,
        ),
        ("dp", "seq", "head"),
    )
    small = lax.psum((grad_conv, grad_beta), everyone)
    sum_mixer = lax.psum_scatter(grad_mixer, everyone, scatter_dimension=1, tiled=True)
    sum_gateup, sum_down = sum_mlp[:2].astype(F32), sum_mlp[2].T.astype(F32)
    sum_qkvg, sum_o = sum_mixer[:4].astype(F32), sum_mixer[4].T.astype(F32)
    state_mean = everywhere[3] / (lax.axis_size("dp") * runs * heads * size)
    return (
        result[None],
        d_tokens[None],
        everywhere[0],
        sum_qkvg,
        small[1],
        small[0],
        everywhere[2],
        sum_o,
        everywhere[1],
        sum_gateup,
        sum_down,
        state_mean,
    )

def solution(mesh):
    rows, halves_of = P("dp", "seq", None), P(None, None, "head")
    placed = (
        rows, P(), halves_of, P(None, "head"), halves_of, P(), P("head", None), P(),
        halves_of, P("head", None), rows,
    )
    shared = P(None, ("dp", "seq"), "head")
    turned = P("head", ("dp", "seq"))
    return jax.shard_map(
        per_device,
        mesh=mesh,
        in_specs=placed,
        out_specs=(
            rows, rows, P(), shared, P(None, "head"), halves_of, P(), turned, P(), shared, turned, P(),
        ),
        check_vma=False,
    )
```
